32 devices in a mesh: seq: 8 (over z, x), tp: 4 (over y, core).
Axes of the slice: x: 2, y: 2, z: 4, core: 2. Of those that a mesh axis runs over, the one named last changes fastest.
Arguments:
- queries: bfloat16 [4096, 4096], P('seq', 'tp'), may hold values from -6 to 6
- keys: bfloat16 [4096, 4096], P('seq', 'tp'), may hold values from -6 to 6
- values: bfloat16 [4096, 4096], P('seq', 'tp'), may hold values from -6 to 6
- log_decay: float32 [4096, 32], P('seq', 'tp'), may hold values from -1.2 to 0, as said below
- out_weight: bfloat16 [4096, 6144], P('tp', 'seq'), may hold values from -0.09375 to 0.09375
- grad_out: bfloat16 [4096, 6144], P('seq', 'tp'), may hold values from -6 to 6
Outputs:
- grad_queries: bfloat16 [4096, 4096], P('seq', 'tp')
- grad_keys: bfloat16 [4096, 4096], P('seq', 'tp')
- grad_values: bfloat16 [4096, 4096], P('seq', 'tp')
- grad_weight: float32 [6144, 4096], P('seq', 'tp')
The draws below stay inside these ranges and needn't reach their ends.
Inputs may be any that keep to these rules, and one draw needn't show every extreme that they name: `log_decay`: log decay of each head's state at each token.
All inputs are finite; a program needn't handle non-finite values.
Results may differ from the reference program's by a relative error of at most 0.0029.
Values may be sent and summed in bfloat16 or wider, within the bound.
A program may use at most 192 MiB of HBM per device.

```python
import math
import jax
import jax.numpy as jnp
from jax import lax

D = 6144
SHARD_ATTN_UNITS = 32
DH = 128
BLOCK = 256
TOK_DEV = 512
STREAM_LENGTH = 4096
HD = 4096


def draw_log_decay(key, part):
    parts_keys = jax.random.split(jax.random.fold_in(key, 17), 6)
    share = 0.5
    fast = jax.random.uniform(parts_keys[0], (SHARD_ATTN_UNITS,)) < share
    fast_rate = jnp.exp(jax.random.uniform(parts_keys[1], (SHARD_ATTN_UNITS,), minval=math.log(1.0 / 50.0), maxval=math.log(1.0 / 30.0)))
    slow_rate = 0.25 / STREAM_LENGTH
    nominal_speed = jnp.where(fast, fast_rate, slow_rate)
    device_blocks = STREAM_LENGTH // TOK_DEV
    processor_factor = jnp.exp(jax.random.uniform(parts_keys[2], (device_blocks, SHARD_ATTN_UNITS), minval=math.log(0.5), maxval=math.log(2.0)))
    processor_factor = jnp.repeat(processor_factor, TOK_DEV, axis=0)
    rough_estimate = jax.random.uniform(parts_keys[3], (STREAM_LENGTH, SHARD_ATTN_UNITS), minval=0.5, maxval=1.5)
    spot_names = jax.random.randint(parts_keys[4], (3, SHARD_ATTN_UNITS), 0, STREAM_LENGTH)
    objective_scores = jax.random.uniform(parts_keys[5], (3, SHARD_ATTN_UNITS), minval=0.6, maxval=0.8)
    word_indices = jnp.arange(STREAM_LENGTH)[:, None]
    spike_occurrences = jnp.zeros((STREAM_LENGTH, SHARD_ATTN_UNITS), jnp.float32)
    for picking_mask in range(3):
        spike_occurrences = spike_occurrences + jnp.where(word_indices == spot_names[picking_mask][None, :], jnp.log(objective_scores[picking_mask])[None, :], 0.0)
    return (spike_occurrences - nominal_speed[None, :] * processor_factor * rough_estimate).astype(jnp.float32)


def raised(array, stream_key, source, target, parts, factor):
    def block_of(dim):
        return (jnp.arange(array.shape[dim]) // (array.shape[dim] // parts)).reshape((-1,) + (1,) * (array.ndim - 1 - dim))

    near = jax.random.permutation(stream_key, parts)[block_of(target)]
    far = (block_of(target) + parts // 2) % parts
    return jnp.where((block_of(source) == near) | (block_of(source) == far), factor * array, array)


def block_scale(stream_key, dims, shards, smallest, high):
    loudness = 1.0
    for dim, parts in shards:
        steps = jax.random.uniform(jax.random.fold_in(jax.random.fold_in(stream_key, 6), dim), (parts,), jnp.float32, smallest / len(shards), high / len(shards))
        loudness = loudness * jnp.repeat(jnp.exp(steps), dims[dim] // parts).reshape((-1,) + (1,) * (len(dims) - 1 - dim))
    return loudness


def noise(own_key, dims, spread, limit, shards=(), held_as=jnp.bfloat16):
    values = spread * jax.random.normal(own_key, dims, jnp.float32)
    if shards:
        values = values * block_scale(own_key, dims, shards, -0.22, 0.18)
    return jnp.clip(values, -limit, limit).astype(held_as)


def noise_with(rng, shape, width, reach, pieces, heavy, dtype=jnp.bfloat16):
    values = width * jax.random.normal(rng, shape, jnp.float32)
    if pieces:
        values = values * block_scale(rng, shape, pieces, -0.22, 0.18)
    return jnp.clip(raised(values, jax.random.fold_in(rng, 3), *heavy), -reach, reach).astype(dtype)


def setup_inputs(seed: int = 0) -> dict:
    seeds = jax.random.split(jax.random.key(seed), 7)
    queries = noise(seeds[0], (STREAM_LENGTH, HD), 1.0, 6.0, ((0, 8), (1, 4)))
    keys = noise(seeds[1], (STREAM_LENGTH, HD), 1.0, 6.0, ((0, 8), (1, 4)))
    values = noise(seeds[2], (STREAM_LENGTH, HD), 1.0, 6.0, ((0, 8), (1, 4)))
    log_decay = draw_log_decay(jax.random.fold_in(seeds[6], 71), 0)
    out_weight = noise(seeds[4], (HD, D), HD ** -0.5, 0.09375, ((0, 4), (1, 8)))
    grad_out = noise_with(seeds[5], (STREAM_LENGTH, D), 1.0, 6.0, ((0, 8), (1, 4)), (0, 1, 8, 2.0))
    return dict(queries=queries, keys=keys, values=values, log_decay=log_decay, out_weight=out_weight, grad_out=grad_out)


EPS = 1e-06
HIGH = lax.Precision.HIGHEST

def attend(query_f, key_f, value_f, rates):
    blocks = query_f.shape[0] // BLOCK
    shape4 = (blocks, BLOCK, SHARD_ATTN_UNITS, DH)
    lower = jnp.arange(BLOCK)[:, None] >= jnp.arange(BLOCK)[None, :]

    def advance(state, item):
        query_b, key_b, value_b, rate_b = item
        cumul = jnp.cumsum(rate_b, axis=0)
        cumul_t = cumul.T
        decay_mat = jnp.where(lower[None], jnp.exp(jnp.minimum(cumul_t[:, :, None] - cumul_t[:, None, :], 0.0)), 0.0)
        scores = jnp.einsum('thd,shd->hts', query_b, key_b, precision=HIGH) * decay_mat
        inner = jnp.einsum('hts,shd->thd', scores, value_b, precision=HIGH)
        outer = jnp.exp(cumul)[:, :, None] * jnp.einsum('thd,hde->the', query_b, state, precision=HIGH)
        total = cumul[-1]
        into_end = jnp.exp(total[None, :] - cumul)
        fresh = jnp.exp(total)[:, None, None] * state + jnp.einsum('th,thd,the->hde', into_end, key_b, value_b, precision=HIGH)
        return (fresh, inner + outer)
    start = jnp.zeros((SHARD_ATTN_UNITS, DH, DH), jnp.float32)
    items = (query_f.reshape(shape4), key_f.reshape(shape4), value_f.reshape(shape4), rates.reshape(blocks, BLOCK, SHARD_ATTN_UNITS))
    final, outputs = lax.scan(jax.checkpoint(advance), start, items)
    return outputs.reshape(STREAM_LENGTH, SHARD_ATTN_UNITS, DH)

def reference(queries, keys, values, log_decay, out_weight, grad_out):
    query_f = queries.astype(jnp.float32).reshape(STREAM_LENGTH, SHARD_ATTN_UNITS, DH)
    key_f = keys.astype(jnp.float32).reshape(STREAM_LENGTH, SHARD_ATTN_UNITS, DH)
    value_f = values.astype(jnp.float32).reshape(STREAM_LENGTH, SHARD_ATTN_UNITS, DH)

    def forward(query_a, key_a, value_a):
        attended = attend(query_a, key_a, value_a, log_decay)
        scale = jnp.sqrt(lax.optimization_barrier(jnp.mean(attended * attended, axis=-1, keepdims=True)) + EPS)
        return attended / scale
    o_hat, pullback = jax.vjp(forward, query_f, key_f, value_f)
    normed = o_hat.reshape(STREAM_LENGTH, HD).astype(jnp.bfloat16)
    grad_normed = jnp.dot(grad_out, out_weight.T, preferred_element_type=jnp.float32)
    grad_q, grad_k, grad_v = pullback(grad_normed.reshape(STREAM_LENGTH, SHARD_ATTN_UNITS, DH))
    grad_weight = jnp.dot(grad_out.T, normed, preferred_element_type=jnp.float32)
    return (grad_q.reshape(STREAM_LENGTH, HD).astype(jnp.bfloat16), grad_k.reshape(STREAM_LENGTH, HD).astype(jnp.bfloat16), grad_v.reshape(STREAM_LENGTH, HD).astype(jnp.bfloat16), grad_weight)
```

```python
import jax
import jax.numpy as jnp
from jax import lax
from jax.experimental import pallas as pl
from jax.experimental.pallas import tpu as pltpu
from jax.sharding import PartitionSpec as P

SUB = 256
EPS = 1e-06
F32 = jnp.float32
BF16 = jnp.bfloat16


def halves(x):
    high = x.astype(BF16)
    return high, (x - high.astype(F32)).astype(BF16)


def dot(a, b, ca, cb):
    return lax.dot_general(a, b, (((ca,), (cb,)), ((), ())), preferred_element_type=F32)


def wide_left(a, b, ca, cb):
    high, low = halves(a)
    return dot(high, b, ca, cb) + dot(low, b, ca, cb)


def wide_right(a, b, ca, cb):
    high, low = halves(b)
    return dot(a, high, ca, cb) + dot(a, low, ca, cb)


def wide_both(a, b, ca, cb):
    ah, al = halves(a)
    bh, bl = halves(b)
    return dot(ah, bh, ca, cb) + (dot(ah, bl, ca, cb) + dot(al, bh, ca, cb))


def decay_between(col, row, diagonal):
    weight = jnp.exp(jnp.minimum(col - row, 0.0))
    if diagonal:
        shape = weight.shape
        lower = lax.broadcasted_iota(jnp.int32, shape, 0) >= lax.broadcasted_iota(jnp.int32, shape, 1)
        weight = jnp.where(lower, weight, 0.0)
    return weight


def state_kernel(k_ref, v_ref, col_ref, state_ref):
    col = col_ref[0]
    total = col[-1:, :]
    state_ref[0] = wide_right(k_ref[...], jnp.exp(total - col) * v_ref[...].astype(F32), 0, 0)


def forward_kernel(q_ref, k_ref, v_ref, col_ref, row_ref, state_ref, att_ref, normed_ref):
    rows = q_ref.shape[0]
    state = state_ref[0]
    for t in range(0, rows, SUB):
        query = q_ref[t : t + SUB, :]
        col = col_ref[0, t : t + SUB, :]
        total = jnp.exp(col) * wide_right(query, state, 1, 0)
        for s in range(0, t + 1, SUB):
            weight = decay_between(col, row_ref[0, :, s : s + SUB], s == t)
            scores = dot(query, k_ref[s : s + SUB, :], 1, 1) * weight
            total = total + wide_left(scores, v_ref[s : s + SUB, :], 1, 0)
        att_ref[t : t + SUB, :] = total
        scale = jnp.sqrt(jnp.mean(total * total, axis=-1, keepdims=True) + EPS)
        normed_ref[t : t + SUB, :] = (total / scale).astype(BF16)


def cotangent_kernel(q_ref, col_ref, att_ref, gn_ref, ga_ref, grad_ref):
    att = att_ref[...]
    scale = jnp.sqrt(jnp.mean(att * att, axis=-1, keepdims=True) + EPS)
    o_hat = att / scale
    gn = gn_ref[...]
    ga = (gn - o_hat * jnp.mean(gn * o_hat, axis=-1, keepdims=True)) / scale
    ga_ref[...] = ga
    grad_ref[0] = wide_right(q_ref[...], jnp.exp(col_ref[0]) * ga, 0, 0)


def backward_kernel(
    q_ref, k_ref, v_ref, ga_ref, col_ref, row_ref, state_ref, end_ref, gq_ref, gk_ref, gv_ref
):
    rows = q_ref.shape[0]
    state = state_ref[0]
    end = end_ref[0]
    col_all = col_ref[0]
    into_end = jnp.exp(col_all[-1:, :] - col_all)
    starts = range(0, rows, SUB)
    gk = {}
    gv = {}
    for s in starts:
        tail = into_end[s : s + SUB, :]
        gk[s] = tail * wide_right(v_ref[s : s + SUB, :], end, 1, 1)
        gv[s] = tail * wide_right(k_ref[s : s + SUB, :], end, 1, 0)
    for t in starts:
        query = q_ref[t : t + SUB, :]
        ga = ga_ref[t : t + SUB, :]
        col = col_all[t : t + SUB, :]
        gq = jnp.exp(col) * wide_both(ga, state, 1, 1)
        for s in range(0, t + 1, SUB):
            key = k_ref[s : s + SUB, :]
            weight = decay_between(col, row_ref[0, :, s : s + SUB], s == t)
            scores = dot(query, key, 1, 1) * weight
            mix = wide_left(ga, v_ref[s : s + SUB, :], 1, 1) * weight
            gq = gq + wide_left(mix, key, 1, 0)
            gk[s] = gk[s] + wide_left(mix, query, 0, 0)
            gv[s] = gv[s] + wide_both(scores, ga, 0, 0)
        gq_ref[t : t + SUB, :] = gq.astype(BF16)
    for s in starts:
        gk_ref[s : s + SUB, :] = gk[s].astype(BF16)
        gv_ref[s : s + SUB, :] = gv[s].astype(BF16)


def per_head(kernel, heads, rows, size, ins, outs, flops):
    kinds = {
        "tok": pl.BlockSpec((rows, size), lambda h: (0, h)),
        "col": pl.BlockSpec((1, rows, 1), lambda h: (h, 0, 0)),
        "row": pl.BlockSpec((1, 1, rows), lambda h: (h, 0, 0)),
        "state": pl.BlockSpec((1, size, size), lambda h: (h, 0, 0)),
    }
    shapes = {"tok": (rows, heads * size), "state": (heads, size, size)}
    return pl.pallas_call(
        kernel,
        grid=(heads,),
        in_specs=[kinds[kind] for kind in ins],
        out_specs=[kinds[kind] for kind, _ in outs],
        out_shape=[jax.ShapeDtypeStruct(shapes[kind], dtype) for kind, dtype in outs],
        compiler_params=pltpu.CompilerParams(vmem_limit_bytes=32 * 2**20),
        cost_estimate=pl.CostEstimate(
            flops=flops, bytes_accessed=4 * rows * heads * size * 2, transcendentals=0
        ),
    )


def on_device(queries, keys, values, log_decay, out_weight, grad_out):
    rows, heads = log_decay.shape
    size = queries.shape[1] // heads
    count, mine = lax.axis_size("seq"), lax.axis_index("seq")
    tps, tp = lax.axis_size("tp"), lax.axis_index("tp")

    cumul = jnp.cumsum(log_decay.T, axis=1)
    row = cumul[:, None, :]
    col = cumul[:, :, None]
    dev_log = cumul[:, -1]
    unit = 2 * rows * heads * size * size
    (dev_state,) = per_head(
        state_kernel, heads, rows, size, ("tok", "tok", "col"), (("state", F32),), 2 * unit
    )(keys, values, col)

    below = jnp.broadcast_to(dev_log[:, None, None], (heads, 8, size))
    pieces = lax.all_gather(jnp.concatenate([dev_state, below], axis=1), "seq")
    logs = pieces[:, :, size, 0]
    place = jnp.arange(count)
    between = (place[None, :] > place[:, None]) & (place[None, :] < mine)
    early = jnp.sum(jnp.where(between[:, :, None], logs[None], 0.0), axis=1)
    early = jnp.where((place < mine)[:, None], jnp.exp(early), 0.0)
    between = (place[None, :] < place[:, None]) & (place[None, :] > mine)
    late = jnp.sum(jnp.where(between[:, :, None], logs[None], 0.0), axis=1)
    late = jnp.where((place > mine)[:, None], jnp.exp(late), 0.0)
    state_in = jnp.sum(early[:, :, None, None] * pieces[:, :, :size, :], axis=0)

    weight_all = lax.all_gather(out_weight, "seq", axis=1, tiled=True)
    cotangent = lax.all_gather(grad_out, "tp", axis=1, tiled=True)

    share = count // tps
    width = grad_out.shape[1] // share
    arrived = jnp.zeros((share, rows, width), grad_out.dtype)
    for turn in range(share):
        pairs = []
        for i in range(count):
            for j in range(tps):
                to = (share * j + (i % share + turn) % share) * tps + i // share
                pairs.append((i * tps + j, to))
        block = lax.rem(lax.rem(mine, share) + turn, share)
        piece = lax.dynamic_slice_in_dim(grad_out, block * width, width, axis=1)
        piece = lax.ppermute(piece, ("seq", "tp"), pairs)
        slot = lax.rem(lax.rem(mine, share) + share - turn, share)
        arrived = lax.dynamic_update_slice_in_dim(arrived, piece[None], slot, axis=0)
    by_columns = lax.all_gather(
        arrived.reshape(share * rows, width), "tp", axis=0, tiled=True
    )

    attended, normed = per_head(
        forward_kernel,
        heads,
        rows,
        size,
        ("tok", "tok", "tok", "col", "row", "state"),
        (("tok", F32), ("tok", BF16)),
        12 * unit,
    )(queries, keys, values, col, row, state_in)
    normed_all = lax.all_gather(normed, "seq", axis=0, tiled=True)

    grad_normed = lax.dot_general(
        cotangent, weight_all, (((1,), (1,)), ((), ())), preferred_element_type=F32
    )
    grad_att, dev_grad = per_head(
        cotangent_kernel,
        heads,
        rows,
        size,
        ("tok", "col", "tok", "tok"),
        (("tok", F32), ("state", F32)),
        2 * unit,
    )(queries, col, attended, grad_normed)
    grads = lax.all_gather(dev_grad, "seq")
    end_grad = jnp.sum(late[:, :, None, None] * grads, axis=0)
    grad_q, grad_k, grad_v = per_head(
        backward_kernel,
        heads,
        rows,
        size,
        ("tok", "tok", "tok", "tok", "col", "row", "state", "state"),
        (("tok", BF16), ("tok", BF16), ("tok", BF16)),
        40 * unit,
    )(queries, keys, values, grad_att, col, row, state_in, end_grad)
    grad_weight = lax.dot_general(
        by_columns, normed_all, (((0,), (0,)), ((), ())), preferred_element_type=F32
    )
    return grad_q, grad_k, grad_v, grad_weight


def solution(mesh):
    spec = P("seq", "tp")
    return jax.shard_map(
        on_device,
        mesh=mesh,
        in_specs=(spec, spec, spec, spec, P("tp", "seq"), spec),
        out_specs=(spec, spec, spec, spec),
        check_vma=False,
    )
```

```python
import jax
import jax.numpy as jnp
from jax import lax
from jax.experimental import pallas as pl
from jax.experimental.pallas import tpu as pltpu
from jax.sharding import PartitionSpec as P

SUB = 256
EPS = 1e-06
F32 = jnp.float32
BF16 = jnp.bfloat16


def halves(x):
    high = x.astype(BF16)
    return high, (x - high.astype(F32)).astype(BF16)


def dot(a, b, ca, cb):
    return lax.dot_general(a, b, (((ca,), (cb,)), ((), ())), preferred_element_type=F32)


def wide_left(a, b, ca, cb):
    high, low = halves(a)
    return dot(high, b, ca, cb) + dot(low, b, ca, cb)


def wide_right(a, b, ca, cb):
    high, low = halves(b)
    return dot(a, high, ca, cb) + dot(a, low, ca, cb)


def wide_both(a, b, ca, cb):
    ah, al = halves(a)
    bh, bl = halves(b)
    return dot(ah, bh, ca, cb) + (dot(ah, bl, ca, cb) + dot(al, bh, ca, cb))


def decay_between(col, row, diagonal):
    weight = jnp.exp(jnp.minimum(col - row, 0.0))
    if diagonal:
        shape = weight.shape
        lower = lax.broadcasted_iota(jnp.int32, shape, 0) >= lax.broadcasted_iota(jnp.int32, shape, 1)
        weight = jnp.where(lower, weight, 0.0)
    return weight


def state_kernel(k_ref, v_ref, col_ref, state_ref):
    col = col_ref[0]
    total = col[-1:, :]
    state_ref[0] = wide_right(k_ref[...], jnp.exp(total - col) * v_ref[...].astype(F32), 0, 0)


def forward_kernel(q_ref, k_ref, v_ref, col_ref, row_ref, state_ref, att_ref, normed_ref):
    rows = q_ref.shape[0]
    state = state_ref[0]
    for t in range(0, rows, SUB):
        query = q_ref[t : t + SUB, :]
        col = col_ref[0, t : t + SUB, :]
        total = jnp.exp(col) * wide_right(query, state, 1, 0)
        for s in range(0, t + 1, SUB):
            weight = decay_between(col, row_ref[0, :, s : s + SUB], s == t)
            scores = dot(query, k_ref[s : s + SUB, :], 1, 1) * weight
            total = total + wide_left(scores, v_ref[s : s + SUB, :], 1, 0)
        att_ref[t : t + SUB, :] = total
        scale = jnp.sqrt(jnp.mean(total * total, axis=-1, keepdims=True) + EPS)
        normed_ref[t : t + SUB, :] = (total / scale).astype(BF16)


def cotangent_kernel(q_ref, col_ref, att_ref, gn_ref, ga_ref, grad_ref):
    att = att_ref[...]
    scale = jnp.sqrt(jnp.mean(att * att, axis=-1, keepdims=True) + EPS)
    o_hat = att / scale
    gn = gn_ref[...]
    ga = (gn - o_hat * jnp.mean(gn * o_hat, axis=-1, keepdims=True)) / scale
    ga_ref[...] = ga
    grad_ref[0] = wide_right(q_ref[...], jnp.exp(col_ref[0]) * ga, 0, 0)


def backward_kernel(
    q_ref, k_ref, v_ref, ga_ref, col_ref, row_ref, state_ref, end_ref, gq_ref, gk_ref, gv_ref
):
    rows = q_ref.shape[0]
    state = state_ref[0]
    end = end_ref[0]
    col_all = col_ref[0]
    into_end = jnp.exp(col_all[-1:, :] - col_all)
    starts = range(0, rows, SUB)
    gk = {}
    gv = {}
    for s in starts:
        tail = into_end[s : s + SUB, :]
        gk[s] = tail * wide_right(v_ref[s : s + SUB, :], end, 1, 1)
        gv[s] = tail * wide_right(k_ref[s : s + SUB, :], end, 1, 0)
    for t in starts:
        query = q_ref[t : t + SUB, :]
        ga = ga_ref[t : t + SUB, :]
        col = col_all[t : t + SUB, :]
        gq = jnp.exp(col) * wide_both(ga, state, 1, 1)
        for s in range(0, t + 1, SUB):
            key = k_ref[s : s + SUB, :]
            weight = decay_between(col, row_ref[0, :, s : s + SUB], s == t)
            scores = dot(query, key, 1, 1) * weight
            mix = wide_left(ga, v_ref[s : s + SUB, :], 1, 1) * weight
            gq = gq + wide_left(mix, key, 1, 0)
            gk[s] = gk[s] + wide_left(mix, query, 0, 0)
            gv[s] = gv[s] + wide_both(scores, ga, 0, 0)
        gq_ref[t : t + SUB, :] = gq.astype(BF16)
    for s in starts:
        gk_ref[s : s + SUB, :] = gk[s].astype(BF16)
        gv_ref[s : s + SUB, :] = gv[s].astype(BF16)


def per_head(kernel, heads, rows, size, ins, outs, flops):
    kinds = {
        "tok": pl.BlockSpec((rows, size), lambda h: (0, h)),
        "col": pl.BlockSpec((1, rows, 1), lambda h: (h, 0, 0)),
        "row": pl.BlockSpec((1, 1, rows), lambda h: (h, 0, 0)),
        "state": pl.BlockSpec((1, size, size), lambda h: (h, 0, 0)),
    }
    shapes = {"tok": (rows, heads * size), "state": (heads, size, size)}
    return pl.pallas_call(
        kernel,
        grid=(heads,),
        in_specs=[kinds[kind] for kind in ins],
        out_specs=[kinds[kind] for kind, _ in outs],
        out_shape=[jax.ShapeDtypeStruct(shapes[kind], dtype) for kind, dtype in outs],
        compiler_params=pltpu.CompilerParams(vmem_limit_bytes=32 * 2**20),
        cost_estimate=pl.CostEstimate(
            flops=flops, bytes_accessed=4 * rows * heads * size * 2, transcendentals=0
        ),
    )


def seq_permute(x, send):
    count = lax.axis_size("seq")
    pairs = [(i, send(i)) for i in range(count)]
    return lax.ppermute(x, "seq", [(i, to) for i, to in pairs if 0 <= to < count])


def seq_blocks(x):
    count, mine = lax.axis_size("seq"), lax.axis_index("seq")
    blocks = []
    for hop in range(count // 2):
        block = seq_permute(x, lambda i: (i + 2 * hop) % count) if hop else x
        place = lax.rem(mine + count - 2 * hop, count)
        blocks.append((place, block))
        other = place + 1 - 2 * lax.rem(place, 2)
        blocks.append((other, seq_permute(block, lambda i: i ^ 1)))
    return blocks


def carried_in(log, state, backward):
    heads, size, _ = state.shape
    count, mine = lax.axis_size("seq"), lax.axis_index("seq")
    side = lax.rem(mine, 2)
    near = (side == 0) if backward else (side == 1)

    def packed(log, state):
        return jnp.concatenate(
            [state, jnp.broadcast_to(log[:, None, None], (heads, 8, size))], axis=1
        )

    def split(pack):
        return pack[:, size, 0], pack[:, :size, :]

    def decayed(log, state):
        return jnp.exp(log)[:, None, None] * state

    pair_log, pair_state = split(seq_permute(packed(log, state), lambda i: i ^ 1))
    both = jnp.where(near, decayed(log, pair_state) + state, decayed(pair_log, state) + pair_state)
    mine_pack = packed(log + pair_log, both)
    total = jnp.zeros_like(state)
    passed = jnp.zeros_like(log)
    for hop in range(1, count // 2):
        step = -2 * hop if backward else 2 * hop
        far_log, far_state = split(seq_permute(mine_pack, lambda i: i + step))
        total = total + decayed(passed, far_state)
        passed = passed + far_log
    return jnp.where(near, decayed(pair_log, total) + pair_state, total)


def on_device(queries, keys, values, log_decay, out_weight, grad_out):
    rows, heads = log_decay.shape
    size = queries.shape[1] // heads
    count, mine = lax.axis_size("seq"), lax.axis_index("seq")
    tps = lax.axis_size("tp")

    cotangent = lax.all_gather(grad_out, "tp", axis=1, tiled=True)
    weight_blocks = seq_blocks(out_weight)

    cumul = jnp.cumsum(log_decay.T, axis=1)
    row = cumul[:, None, :]
    col = cumul[:, :, None]
    dev_log = cumul[:, -1]
    unit = 2 * rows * heads * size * size
    (dev_state,) = per_head(
        state_kernel, heads, rows, size, ("tok", "tok", "col"), (("state", F32),), 2 * unit
    )(keys, values, col)
    state_in = carried_in(dev_log, dev_state, False)

    share = count // tps
    width = grad_out.shape[1] // share
    arrived = jnp.zeros((share, rows, width), grad_out.dtype)
    for turn in range(share):
        pairs = []
        for i in range(count):
            for j in range(tps):
                to = (share * j + (i % share + turn) % share) * tps + i // share
                pairs.append((i * tps + j, to))
        block = lax.rem(lax.rem(mine, share) + turn, share)
        piece = lax.dynamic_slice_in_dim(grad_out, block * width, width, axis=1)
        piece = lax.ppermute(piece, ("seq", "tp"), pairs)
        slot = lax.rem(lax.rem(mine, share) + share - turn, share)
        arrived = lax.dynamic_update_slice_in_dim(arrived, piece[None], slot, axis=0)
    by_columns = lax.all_gather(
        arrived.reshape(share * rows, width), "tp", axis=0, tiled=True
    )

    attended, normed = per_head(
        forward_kernel,
        heads,
        rows,
        size,
        ("tok", "tok", "tok", "col", "row", "state"),
        (("tok", F32), ("tok", BF16)),
        12 * unit,
    )(queries, keys, values, col, row, state_in)
    normed_blocks = seq_blocks(normed)

    grad_normed = jnp.zeros((rows, heads * size), F32)
    for place, block in weight_blocks:
        part = lax.dynamic_slice_in_dim(cotangent, place * width, width, axis=1)
        grad_normed = grad_normed + lax.dot_general(
            part, block, (((1,), (1,)), ((), ())), preferred_element_type=F32
        )
    grad_att, dev_grad = per_head(
        cotangent_kernel,
        heads,
        rows,
        size,
        ("tok", "col", "tok", "tok"),
        (("tok", F32), ("state", F32)),
        2 * unit,
    )(queries, col, attended, grad_normed)
    end_grad = carried_in(dev_log, dev_grad, True)
    grad_q, grad_k, grad_v = per_head(
        backward_kernel,
        heads,
        rows,
        size,
        ("tok", "tok", "tok", "tok", "col", "row", "state", "state"),
        (("tok", BF16), ("tok", BF16), ("tok", BF16)),
        40 * unit,
    )(queries, keys, values, grad_att, col, row, state_in, end_grad)
    grad_weight = jnp.zeros((width, heads * size), F32)
    for place, block in normed_blocks:
        part = lax.dynamic_slice_in_dim(by_columns, place * rows, rows, axis=0)
        grad_weight = grad_weight + lax.dot_general(
            part, block, (((0,), (0,)), ((), ())), preferred_element_type=F32
        )
    return grad_q, grad_k, grad_v, grad_weight


def solution(mesh):
    spec = P("seq", "tp")
    return jax.shard_map(
        on_device,
        mesh=mesh,
        in_specs=(spec, spec, spec, spec, P("tp", "seq"), spec),
        out_specs=(spec, spec, spec, spec),
        check_vma=False,
    )
```

```python
import jax
import jax.numpy as jnp
from jax import lax
from jax.experimental import pallas as pl
from jax.experimental.pallas import tpu as pltpu
from jax.sharding import PartitionSpec as P

SUB = 256
EPS = 1e-06
F32 = jnp.float32
BF16 = jnp.bfloat16


def halves(x):
    high = x.astype(BF16)
    return high, (x - high.astype(F32)).astype(BF16)


def dot(a, b, ca, cb):
    return lax.dot_general(a, b, (((ca,), (cb,)), ((), ())), preferred_element_type=F32)


def wide_left(a, b, ca, cb):
    high, low = halves(a)
    return dot(high, b, ca, cb) + dot(low, b, ca, cb)


def wide_right(a, b, ca, cb):
    high, low = halves(b)
    return dot(a, high, ca, cb) + dot(a, low, ca, cb)


def wide_both(a, b, ca, cb):
    ah, al = halves(a)
    bh, bl = halves(b)
    return dot(ah, bh, ca, cb) + (dot(ah, bl, ca, cb) + dot(al, bh, ca, cb))


def decay_between(col, row, diagonal):
    weight = jnp.exp(jnp.minimum(col - row, 0.0))
    if diagonal:
        shape = weight.shape
        lower = lax.broadcasted_iota(jnp.int32, shape, 0) >= lax.broadcasted_iota(jnp.int32, shape, 1)
        weight = jnp.where(lower, weight, 0.0)
    return weight


def state_kernel(k_ref, v_ref, col_ref, state_ref):
    col = col_ref[0]
    total = col[-1:, :]
    state_ref[0] = wide_right(k_ref[...], jnp.exp(total - col) * v_ref[...].astype(F32), 0, 0)


def forward_kernel(q_ref, k_ref, v_ref, col_ref, row_ref, state_ref, att_ref, normed_ref):
    rows = q_ref.shape[0]
    state = state_ref[0]
    for t in range(0, rows, SUB):
        query = q_ref[t : t + SUB, :]
        col = col_ref[0, t : t + SUB, :]
        total = jnp.exp(col) * wide_right(query, state, 1, 0)
        for s in range(0, t + 1, SUB):
            weight = decay_between(col, row_ref[0, :, s : s + SUB], s == t)
            scores = dot(query, k_ref[s : s + SUB, :], 1, 1) * weight
            total = total + wide_left(scores, v_ref[s : s + SUB, :], 1, 0)
        att_ref[t : t + SUB, :] = total
        scale = jnp.sqrt(jnp.mean(total * total, axis=-1, keepdims=True) + EPS)
        normed_ref[t : t + SUB, :] = (total / scale).astype(BF16)


def cotangent_kernel(q_ref, col_ref, att_ref, gn_ref, ga_ref, grad_ref):
    att = att_ref[...]
    scale = jnp.sqrt(jnp.mean(att * att, axis=-1, keepdims=True) + EPS)
    o_hat = att / scale
    gn = gn_ref[...]
    ga = (gn - o_hat * jnp.mean(gn * o_hat, axis=-1, keepdims=True)) / scale
    ga_ref[...] = ga
    grad_ref[0] = wide_right(q_ref[...], jnp.exp(col_ref[0]) * ga, 0, 0)


def backward_kernel(
    q_ref, k_ref, v_ref, ga_ref, col_ref, row_ref, state_ref, end_ref, gq_ref, gk_ref, gv_ref
):
    rows = q_ref.shape[0]
    state = state_ref[0]
    end = end_ref[0]
    col_all = col_ref[0]
    into_end = jnp.exp(col_all[-1:, :] - col_all)
    starts = range(0, rows, SUB)
    gk = {}
    gv = {}
    for s in starts:
        tail = into_end[s : s + SUB, :]
        gk[s] = tail * wide_right(v_ref[s : s + SUB, :], end, 1, 1)
        gv[s] = tail * wide_right(k_ref[s : s + SUB, :], end, 1, 0)
    for t in starts:
        query = q_ref[t : t + SUB, :]
        ga = ga_ref[t : t + SUB, :]
        col = col_all[t : t + SUB, :]
        gq = jnp.exp(col) * wide_both(ga, state, 1, 1)
        for s in range(0, t + 1, SUB):
            key = k_ref[s : s + SUB, :]
            weight = decay_between(col, row_ref[0, :, s : s + SUB], s == t)
            scores = dot(query, key, 1, 1) * weight
            mix = wide_left(ga, v_ref[s : s + SUB, :], 1, 1) * weight
            gq = gq + wide_left(mix, key, 1, 0)
            gk[s] = gk[s] + wide_left(mix, query, 0, 0)
            gv[s] = gv[s] + wide_both(scores, ga, 0, 0)
        gq_ref[t : t + SUB, :] = gq.astype(BF16)
    for s in starts:
        gk_ref[s : s + SUB, :] = gk[s].astype(BF16)
        gv_ref[s : s + SUB, :] = gv[s].astype(BF16)


def per_head(kernel, heads, rows, size, ins, outs, flops):
    kinds = {
        "tok": pl.BlockSpec((rows, size), lambda h: (0, h)),
        "col": pl.BlockSpec((1, rows, 1), lambda h: (h, 0, 0)),
        "row": pl.BlockSpec((1, 1, rows), lambda h: (h, 0, 0)),
        "state": pl.BlockSpec((1, size, size), lambda h: (h, 0, 0)),
    }
    shapes = {"tok": (rows, heads * size), "state": (heads, size, size)}
    return pl.pallas_call(
        kernel,
        grid=(heads,),
        in_specs=[kinds[kind] for kind in ins],
        out_specs=[kinds[kind] for kind, _ in outs],
        out_shape=[jax.ShapeDtypeStruct(shapes[kind], dtype) for kind, dtype in outs],
        compiler_params=pltpu.CompilerParams(vmem_limit_bytes=32 * 2**20),
        cost_estimate=pl.CostEstimate(
            flops=flops, bytes_accessed=4 * rows * heads * size * 2, transcendentals=0
        ),
    )


def seq_permute(x, send):
    count = lax.axis_size("seq")
    pairs = [(i, send(i)) for i in range(count)]
    return lax.ppermute(x, "seq", [(i, to) for i, to in pairs if 0 <= to < count])


def tp_blocks(x):
    count, mine = lax.axis_size("tp"), lax.axis_index("tp")
    blocks = []
    for hop in range(count // 2):
        block = x
        if hop:
            block = lax.ppermute(x, "tp", [(i, (i + 2 * hop) % count) for i in range(count)])
        place = lax.rem(mine + count - 2 * hop, count)
        blocks.append((place, block))
        other = place + 1 - 2 * lax.rem(place, 2)
        blocks.append((other, lax.ppermute(block, "tp", [(i, i ^ 1) for i in range(count)])))
    return blocks


def carried_in(log, state, backward):
    heads, size, _ = state.shape
    count, mine = lax.axis_size("seq"), lax.axis_index("seq")
    side = lax.rem(mine, 2)
    near = (side == 0) if backward else (side == 1)

    def packed(log, state):
        return jnp.concatenate(
            [state, jnp.broadcast_to(log[:, None, None], (heads, 8, size))], axis=1
        )

    def split(pack):
        return pack[:, size, 0], pack[:, :size, :]

    def decayed(log, state):
        return jnp.exp(log)[:, None, None] * state

    pair_log, pair_state = split(seq_permute(packed(log, state), lambda i: i ^ 1))
    both = jnp.where(near, decayed(log, pair_state) + state, decayed(pair_log, state) + pair_state)
    mine_pack = packed(log + pair_log, both)
    total = jnp.zeros_like(state)
    passed = jnp.zeros_like(log)
    for hop in range(1, count // 2):
        step = -2 * hop if backward else 2 * hop
        far_log, far_state = split(seq_permute(mine_pack, lambda i: i + step))
        total = total + decayed(passed, far_state)
        passed = passed + far_log
    return jnp.where(near, decayed(pair_log, total) + pair_state, total)


def on_device(queries, keys, values, log_decay, out_weight, grad_out):
    rows, heads = log_decay.shape
    size = queries.shape[1] // heads
    count, mine = lax.axis_size("seq"), lax.axis_index("seq")
    tps = lax.axis_size("tp")

    weight_all = lax.all_gather(out_weight, "seq", axis=1, tiled=True)
    cotangent = tp_blocks(grad_out)

    cumul = jnp.cumsum(log_decay.T, axis=1)
    row = cumul[:, None, :]
    col = cumul[:, :, None]
    dev_log = cumul[:, -1]
    unit = 2 * rows * heads * size * size
    (dev_state,) = per_head(
        state_kernel, heads, rows, size, ("tok", "tok", "col"), (("state", F32),), 2 * unit
    )(keys, values, col)
    state_in = carried_in(dev_log, dev_state, False)

    grad_out, state_in = lax.optimization_barrier((grad_out, state_in))
    share = count // tps
    width = grad_out.shape[1] // share
    arrived = jnp.zeros((share, rows, width), grad_out.dtype)
    for turn in range(share):
        pairs = []
        for i in range(count):
            for j in range(tps):
                to = (share * j + (i % share + turn) % share) * tps + i // share
                pairs.append((i * tps + j, to))
        block = lax.rem(lax.rem(mine, share) + turn, share)
        piece = lax.dynamic_slice_in_dim(grad_out, block * width, width, axis=1)
        piece = lax.ppermute(piece, ("seq", "tp"), pairs)
        slot = lax.rem(lax.rem(mine, share) + share - turn, share)
        arrived = lax.dynamic_update_slice_in_dim(arrived, piece[None], slot, axis=0)
    by_columns = tp_blocks(arrived.reshape(share * rows, width))

    attended, normed = per_head(
        forward_kernel,
        heads,
        rows,
        size,
        ("tok", "tok", "tok", "col", "row", "state"),
        (("tok", F32), ("tok", BF16)),
        12 * unit,
    )(queries, keys, values, col, row, state_in)
    own_cot, own_columns = [cotangent[0][1]], [by_columns[0][1]]
    normed, weight_all, late_cot, late_columns = lax.optimization_barrier(
        (
            normed,
            weight_all,
            [block for _, block in cotangent[1:]],
            [block for _, block in by_columns[1:]],
        )
    )
    cotangent = [(at, x) for (at, _), x in zip(cotangent, own_cot + late_cot)]
    by_columns = [(at, x) for (at, _), x in zip(by_columns, own_columns + late_columns)]
    normed_all = lax.all_gather(normed, "seq", axis=0, tiled=True)

    grad_normed = jnp.zeros((rows, heads * size), F32)
    for place, block in cotangent:
        part = lax.dynamic_slice_in_dim(weight_all, place * share * width, share * width, axis=1)
        grad_normed = grad_normed + lax.dot_general(
            block, part, (((1,), (1,)), ((), ())), preferred_element_type=F32
        )
    grad_att, dev_grad = per_head(
        cotangent_kernel,
        heads,
        rows,
        size,
        ("tok", "col", "tok", "tok"),
        (("tok", F32), ("state", F32)),
        2 * unit,
    )(queries, col, attended, grad_normed)
    end_grad = carried_in(dev_log, dev_grad, True)
    grad_q, grad_k, grad_v = per_head(
        backward_kernel,
        heads,
        rows,
        size,
        ("tok", "tok", "tok", "tok", "col", "row", "state", "state"),
        (("tok", BF16), ("tok", BF16), ("tok", BF16)),
        40 * unit,
    )(queries, keys, values, grad_att, col, row, state_in, end_grad)
    grad_weight = jnp.zeros((width, heads * size), F32)
    for place, block in by_columns:
        part = lax.dynamic_slice_in_dim(normed_all, place * share * rows, share * rows, axis=0)
        grad_weight = grad_weight + lax.dot_general(
            block, part, (((0,), (0,)), ((), ())), preferred_element_type=F32
        )
    return grad_q, grad_k, grad_v, grad_weight


def solution(mesh):
    spec = P("seq", "tp")
    return jax.shard_map(
        on_device,
        mesh=mesh,
        in_specs=(spec, spec, spec, spec, P("tp", "seq"), spec),
        out_specs=(spec, spec, spec, spec),
        check_vma=False,
    )
```
